32 devices in a mesh: section: 2 (over core), tensor: 4 (over y, x), dp: 4 (over z).
Axes of the slice: x: 2, y: 2, z: 4, core: 2. Of those that a mesh axis runs over, the one named last changes fastest.
Arguments:
- layer_input: bfloat16 [2, 4, 1024, 1024], P(None, 'dp', 'tensor'), may hold values from -6 to 6
- cotangent: bfloat16 [2, 4, 1024, 1024], P(None, 'dp', 'tensor'), may hold values from -6 to 6
- segment_ids: int32 [2, 4, 1024], P(None, 'dp'), may hold values from 0 to 1023, as said below
- positions: int32 [2, 4, 1024], P(None, 'dp'), may hold values from 0 to 1023, as said below
- attention_gain: float32 [2, 1024], P('section'), may hold values from 0.25 to 1.75
- attention_in_weight: bfloat16 [2, 1024, 3, 1024], P('section', 'dp', None, 'tensor'), may hold values from -0.1875 to 0.1875
- attention_out_weight: bfloat16 [2, 1024, 1024], P('section', ('tensor', 'dp')), may hold values from -0.75 to 0.75
- feedforward_gain: float32 [2, 1024], P('section'), may hold values from 0.25 to 1.75
- gate_up_weight: bfloat16 [2, 1024, 2, 2624], P('section', 'dp', None, 'tensor'), may hold values from -0.1875 to 0.1875
- down_weight: bfloat16 [2, 2624, 1024], P('section', ('tensor', 'dp')), may hold values from -0.125 to 0.125
Outputs:
- hidden_states: bfloat16 [2, 2, 4, 1024, 1024], P('section', None, 'dp', 'tensor')
- input_grads: float32 [2, 2, 4, 1024, 1024], P('section', None, 'dp', 'tensor')
- grad_attention_gain: float32 [2, 1024], P('section', ('tensor', 'dp'))
- grad_attention_in: float32 [2, 1024, 3, 1024], P('section', 'dp', None, 'tensor')
- grad_attention_out: float32 [2, 1024, 1024], P('section', ('tensor', 'dp'))
- grad_feedforward_gain: float32 [2, 1024], P('section', ('tensor', 'dp'))
- grad_gate_up: float32 [2, 1024, 2, 2624], P('section', 'dp', None, 'tensor')
- grad_down: float32 [2, 2624, 1024], P('section', ('tensor', 'dp'))
The draws below stay inside these ranges and needn't reach their ends.
Inputs may be any that keep to these rules, and one draw needn't show every extreme that they name: `segment_ids`: within a sequence segment numbers start at 0 and rise by one at each document's first token. `positions`: positions count from 0 at each document's first token, as segment_ids gives the documents.
All inputs are finite; a program needn't handle non-finite values.
Results may differ from the reference program's by a relative error of at most 0.039.
Values may be sent and summed in bfloat16 or wider, within the bound.
No kernel may reach another device: no remote copies, remote signals or barrier semaphores. Data moves between devices by JAX's collectives and lax.ppermute only.
A program may use at most 192 MiB of HBM per device.

```python
import math
import jax
import jax.numpy as jnp
from jax import lax

D = 1024
HEADS = 16
HEAD_DIM = 64
FF = 2624
HHD = 1024
SEQ_LEN = 1024
MICRO = 2
SEQS = 4
N_SECTION = 2


def document_starts(base_key):
    draw_key = jax.random.fold_in(base_key, 11)
    rate_key, pick_key = jax.random.split(draw_key)
    exponent = jax.random.randint(rate_key, (MICRO, SEQS, 16), 1, 11)
    rate_rows = jnp.left_shift(jnp.ones_like(exponent), exponent)
    rate_rows = jnp.repeat(rate_rows, SEQ_LEN // 16, axis=2)
    pick_values = jax.random.randint(pick_key, (MICRO, SEQS, SEQ_LEN), 0, 1 << 20)
    indices = jnp.arange(SEQ_LEN, dtype=jnp.int32)
    start_flags = jnp.logical_or(pick_values % rate_rows == 0, indices[None, None, :] == 0)
    micro_index = jnp.arange(MICRO, dtype=jnp.int32)[:, None, None]
    seq_index = jnp.arange(SEQS, dtype=jnp.int32)[None, :, None]
    single_doc = jnp.logical_and(micro_index == 0, seq_index == 0)
    every_token = jnp.logical_and(micro_index == MICRO - 1, seq_index == SEQS - 1)
    start_flags = jnp.where(single_doc, indices[None, None, :] == 0, start_flags)
    start_flags = jnp.logical_or(start_flags, jnp.logical_and(every_token, indices[None, None, :] >= 0))
    return (start_flags.astype(jnp.int32), indices)


def draw_segment_ids(key, part):
    start_flags, indices = document_starts(key)
    return (jnp.cumsum(start_flags, axis=2) - 1).astype(jnp.int32)


def draw_positions(key, part):
    start_flags, indices = document_starts(key)
    begins = lax.cummax(jnp.where(start_flags > 0, indices[None, None, :], 0), axis=2)
    return (indices[None, None, :] - begins).astype(jnp.int32)


def strengthened(drawn, own_key, source, target, parts, factor):
    def block_of(axis_at):
        return (jnp.arange(drawn.shape[axis_at]) // (drawn.shape[axis_at] // parts)).reshape((-1,) + (1,) * (drawn.ndim - 1 - axis_at))

    near = jax.random.permutation(own_key, parts)[block_of(target)]
    other_side = (block_of(target) + parts // 2) % parts
    return jnp.where((block_of(source) == near) | (block_of(source) == other_side), factor * drawn, drawn)


def steps_of(key, shape, cuts, smallest, high):
    def one(dim, shards_of):
        steps = jax.random.uniform(jax.random.fold_in(jax.random.fold_in(key, 6), dim), (shards_of,), jnp.float32, smallest / len(cuts), high / len(cuts))
        return jnp.repeat(jnp.exp(steps), shape[dim] // shards_of).reshape((-1,) + (1,) * (len(shape) - dim - 1))

    factor_of = one(*cuts[0])
    for cut in cuts[1:]:
        factor_of = factor_of * one(*cut)
    return factor_of


def scatter_about(own_key, extent, spread, bound, shards=(), kind=jnp.bfloat16):
    drawn = jax.random.normal(own_key, extent, jnp.float32) * spread
    if len(shards) > 0:
        drawn = steps_of(own_key, extent, shards, -0.22, 0.18) * drawn
    return jnp.clip(drawn, min=-bound, max=bound).astype(kind)


def heavy_noise(stream_key, dims, deviation, limit, shards, heavy, kind=jnp.bfloat16):
    array = deviation * jax.random.normal(stream_key, dims, jnp.float32)
    if shards:
        array = array * steps_of(stream_key, dims, shards, -0.22, 0.18)
    return jnp.clip(strengthened(array, jax.random.fold_in(stream_key, 3), *heavy), -limit, limit).astype(kind)


def setup_inputs(seed: int = 0) -> dict:
    key_of = jax.random.split(jax.random.key(seed), 11)
    return {
        "layer_input": scatter_about(key_of[0], (MICRO, SEQS, SEQ_LEN, D), 1.0, 6.0, ((1, 4), (2, 4))),
        "cotangent": heavy_noise(key_of[1], (MICRO, SEQS, SEQ_LEN, D), 1.0, 6.0, ((1, 4), (2, 4)), (1, 3, 4, 2.0)),
        "segment_ids": draw_segment_ids(jax.random.fold_in(key_of[10], 71), 0),
        "positions": draw_positions(jax.random.fold_in(key_of[10], 71), 0),
        "attention_gain": jnp.clip(1.0 + 0.15 * jax.random.normal(key_of[4], (N_SECTION, D), jnp.float32), 0.25, 1.75),
        "attention_in_weight": scatter_about(key_of[5], (N_SECTION, D, 3, HHD), D ** -0.5, 0.1875, ((0, 2), (1, 4), (3, 4))),
        "attention_out_weight": scatter_about(key_of[6], (N_SECTION, HHD, D), (HHD // 16) ** -0.5, 0.75, ((0, 2), (1, 16))),
        "feedforward_gain": jnp.clip(1.0 + 0.15 * jax.random.normal(key_of[7], (N_SECTION, D), jnp.float32), 0.25, 1.75),
        "gate_up_weight": scatter_about(key_of[8], (N_SECTION, D, 2, FF), D ** -0.5, 0.1875, ((0, 2), (1, 4), (3, 4))),
        "down_weight": scatter_about(key_of[9], (N_SECTION, FF, D), FF ** -0.5, 0.125, ((0, 2), (1, 16))),
    }


EPSILON = 1e-05
THETA = 160000.0
NEGATIVE = -1000000000.0
HIGHEST = lax.Precision.HIGHEST

@jax.custom_vjp
def low(v):
    return lax.optimization_barrier(v.astype(jnp.bfloat16)).astype(jnp.float32)

@jax.custom_vjp
def low_back(v):
    return v

def low_keep(v):
    return (low(v), None)

def low_pass(kept, grad):
    return (grad,)

def back_keep(v):
    return (v, None)

def back_low(kept, grad):
    return (low(grad),)
low.defvjp(low_keep, low_pass)
low_back.defvjp(back_keep, back_low)

def layer_norm(values, gain_vector):
    centered = values - lax.optimization_barrier(jnp.mean(values, -1, keepdims=True))
    variance = lax.optimization_barrier(jnp.mean(centered * centered, -1, keepdims=True))
    return centered * lax.rsqrt(variance + EPSILON) * gain_vector

def rotary_tables(position_row, head_width):
    half_width = head_width // 2
    frequency = THETA ** (-(jnp.arange(half_width, dtype=jnp.float32) * 2.0) / head_width)
    angles = position_row.astype(jnp.float32)[:, None] * frequency[None, :]
    return (jnp.cos(angles)[:, None, :], jnp.sin(angles)[:, None, :])

def rotate(values, cosine, sine_table):
    half_width = values.shape[-1] // 2
    first_half = values[..., :half_width]
    second_half = values[..., half_width:]
    return jnp.concatenate([first_half * cosine - second_half * sine_table, second_half * cosine + first_half * sine_table], -1)

def attention(queries, key_rows, value_rows, segments):
    length = queries.shape[0]
    block_rows = min(512, length)
    block_count = length // block_rows
    score_scale = 1.0 / math.sqrt(queries.shape[-1])
    query_blocks = queries.reshape(block_count, block_rows, queries.shape[1], queries.shape[2])
    segment_blocks = segments.reshape(block_count, block_rows)

    def one_block(operands):
        block_queries, block_segments = operands
        scores = low_back(jnp.einsum('qhe,khe->hqk', block_queries, key_rows, precision=HIGHEST) * score_scale)
        allowed = block_segments[:, None] == segments[None, :]
        scores = jnp.where(allowed[None], scores, NEGATIVE)
        largest = lax.optimization_barrier(jnp.max(scores, -1, keepdims=True))
        exponent = jnp.exp(scores - largest)
        weights_low = low(exponent / lax.optimization_barrier(jnp.sum(exponent, -1, keepdims=True)))
        return jnp.einsum('hqk,khe->qhe', weights_low, value_rows, precision=HIGHEST)
    mixed_rows = lax.map(jax.checkpoint(one_block), (query_blocks, segment_blocks))
    return mixed_rows.reshape(length, queries.shape[1] * queries.shape[2])

def residual_layer(inputs, segments, position_row, attention_gain, attention_in, attention_out, feedforward_gain, gate_up, down_proj):
    length = inputs.shape[0]
    normed = low(layer_norm(inputs, attention_gain))
    projected = low_back(jnp.dot(normed, attention_in.reshape(D, 3 * HHD), precision=HIGHEST))
    projected = projected.reshape(length, 3, HEADS, HEAD_DIM)
    cosine, sine_table = rotary_tables(position_row, HEAD_DIM)
    queries = low(rotate(projected[:, 0], cosine, sine_table))
    key_rows = low(rotate(projected[:, 1], cosine, sine_table))
    value_rows = low(projected[:, 2])
    mixed_rows = low(low_back(attention(queries, key_rows, value_rows, segments)))
    branch = low_back(jnp.dot(mixed_rows, attention_out, precision=HIGHEST))
    middle = inputs + branch
    hidden_in = low(layer_norm(middle, feedforward_gain))
    gate_values = low_back(jnp.dot(hidden_in, gate_up.reshape(D, 2 * FF), precision=HIGHEST)).reshape(length, 2, FF)
    activated = low(jax.nn.gelu(gate_values[:, 0], approximate=False) * gate_values[:, 1])
    return middle + low_back(jnp.dot(activated, down_proj, precision=HIGHEST))

def reference(layer_input, cotangent, segment_ids, positions, attention_gain, attention_in_weight, attention_out_weight, feedforward_gain, gate_up_weight, down_weight):
    weights = tuple((weight_item.astype(jnp.float32) for weight_item in (attention_gain, attention_in_weight, attention_out_weight, feedforward_gain, gate_up_weight, down_weight)))
    sequence_count = MICRO * SEQS
    inputs = layer_input.astype(jnp.float32).reshape(sequence_count, SEQ_LEN, D)
    cotangents = cotangent.astype(jnp.float32).reshape(sequence_count, SEQ_LEN, D)
    segment_rows = segment_ids.reshape(sequence_count, SEQ_LEN)
    position_rows = positions.reshape(sequence_count, SEQ_LEN)
    first_weights = tuple((weight_item[0] for weight_item in weights))
    second_weights = tuple((weight_item[1] for weight_item in weights))
    zeros_first = tuple((jnp.zeros_like(weight_item) for weight_item in first_weights))
    zeros_second = tuple((jnp.zeros_like(weight_item) for weight_item in second_weights))

    def one_sequence(grad_sums, operands):
        sums_first, sums_second = grad_sums
        sequence_in, sequence_cot, sequence_segments, sequence_positions = operands

        def section_one(values, *params):
            return low(residual_layer(values, sequence_segments, sequence_positions, *params))

        def section_two(values, *params):
            return residual_layer(values, sequence_segments, sequence_positions, *params)
        middle_out, back_one = jax.vjp(section_one, sequence_in, *first_weights)
        final_out, back_two = jax.vjp(section_two, middle_out, *second_weights)
        grads_two = back_two(sequence_cot)
        grads_one = back_one(low(grads_two[0]))
        sums_first = tuple((left_sum + right_sum for left_sum, right_sum in zip(sums_first, grads_one[1:])))
        sums_second = tuple((left_sum + right_sum for left_sum, right_sum in zip(sums_second, grads_two[1:])))
        return ((sums_first, sums_second), (middle_out, final_out, grads_one[0], grads_two[0]))
    totals, stacked = lax.scan(one_sequence, (zeros_first, zeros_second), (inputs, cotangents, segment_rows, position_rows))
    sums_first, sums_second = totals
    middle_all, final_all, grad_in_all, grad_mid_all = stacked
    full_shape = (MICRO, SEQS, SEQ_LEN, D)
    hidden_states = jnp.stack([middle_all.reshape(full_shape), final_all.reshape(full_shape)]).astype(jnp.bfloat16)
    input_grads = jnp.stack([grad_in_all.reshape(full_shape), grad_mid_all.reshape(full_shape)])
    grads = tuple((jnp.stack([first_item, second_item]) for first_item, second_item in zip(sums_first, sums_second)))
    return (hidden_states, input_grads, grads[0], grads[1], grads[2], grads[3], grads[4], grads[5])
```

```python
import math

import jax
import jax.numpy as jnp
from jax import lax
from jax.sharding import PartitionSpec as P

HEAD_DIM = 64
EPSILON = 1e-05
THETA = 160000.0
NEGATIVE = -1000000000.0
F32 = jnp.float32
BF16 = jnp.bfloat16

NEAR = [(i, i ^ 1) for i in range(4)]
FAR = [(i, i ^ 2) for i in range(4)]
CORES = [(0, 1), (1, 0)]


def near(block):
    return lax.ppermute(block, "tensor", NEAR)


def far(block):
    return lax.ppermute(block, "tensor", FAR)


def swap(block):
    return lax.ppermute(block, "section", CORES)


def gather_rows(own):
    half = own.shape[0] // 2
    top, bottom = own[:half], own[half:]
    near_top, far_bottom = near(top), far(bottom)
    near_bottom, far_top = near(bottom), far(top)
    diag_top, diag_bottom = far(near_top), near(far_bottom)
    return jnp.concatenate(
        [own, near_top, near_bottom, far_top, far_bottom, diag_top, diag_bottom], 0
    )


def scatter_rows(part):
    half = part.shape[0] // 8
    piece = [part[i * half : (i + 1) * half] for i in range(8)]
    diag_top, diag_bottom = near(piece[6]), far(piece[7])
    near_top, far_bottom = near(piece[2]), far(piece[5])
    far_top = far((piece[4].astype(F32) + diag_top.astype(F32)).astype(BF16))
    near_bottom = near((piece[3].astype(F32) + diag_bottom.astype(F32)).astype(BF16))
    top = piece[0].astype(F32) + near_top.astype(F32) + far_top.astype(F32)
    bottom = piece[1].astype(F32) + near_bottom.astype(F32) + far_bottom.astype(F32)
    return jnp.concatenate([top, bottom], 0)


def slot_order(row, t):
    size = row.shape[0] // 4
    return jnp.concatenate(
        [lax.dynamic_slice_in_dim(row, (t ^ m) * size, size) for m in range(4)], 0
    )


def norm_parts(values):
    centered = values - jnp.mean(values, -1, keepdims=True)
    inverse = lax.rsqrt(jnp.mean(centered * centered, -1, keepdims=True) + EPSILON)
    return centered * inverse, inverse


def layer_norm(values, gain):
    return (norm_parts(values)[0] * gain).astype(BF16)


def norm_back(values, gain, grad):
    normed, inverse = norm_parts(values)
    gain_grad = jnp.sum(grad * normed, 0)
    scaled = grad * gain
    back = inverse * (
        scaled
        - jnp.mean(scaled, -1, keepdims=True)
        - normed * jnp.mean(scaled * normed, -1, keepdims=True)
    )
    return back, gain_grad


def rotary_tables(position_row):
    half_width = HEAD_DIM // 2
    frequency = THETA ** (-(jnp.arange(half_width, dtype=F32) * 2.0) / HEAD_DIM)
    angles = position_row.astype(F32)[:, None] * frequency[None, :]
    return (jnp.cos(angles)[:, None, :], jnp.sin(angles)[:, None, :])


def rotate(values, cosine, sine_table):
    half_width = values.shape[-1] // 2
    first_half = values[..., :half_width]
    second_half = values[..., half_width:]
    return jnp.concatenate(
        [
            first_half * cosine - second_half * sine_table,
            second_half * cosine + first_half * sine_table,
        ],
        -1,
    )


def dot(a, b):
    return jnp.dot(a, b, preferred_element_type=F32)


def dot_nt(a, b):
    return lax.dot_general(a, b, (((1,), (1,)), ((), ())), preferred_element_type=F32)


def dot_tn(a, b):
    return lax.dot_general(a, b, (((0,), (0,)), ((), ())), preferred_element_type=F32)


def masked_scores(queries, key_rows, allowed):
    scores = jnp.einsum("qhe,khe->hqk", queries, key_rows, preferred_element_type=F32)
    return jnp.where(allowed, scores * (1.0 / math.sqrt(HEAD_DIM)), NEGATIVE)


def attention_forward(queries, key_rows, value_rows, segments):
    allowed = (segments[:, None] == segments[None, :])[None]
    scores = masked_scores(queries, key_rows, allowed)
    largest = jnp.max(scores, -1, keepdims=True)
    exponent = jnp.exp(scores - largest)
    total = jnp.sum(exponent, -1, keepdims=True)
    weights = (exponent / total).astype(BF16)
    mixed = jnp.einsum("hqk,khe->qhe", weights, value_rows, preferred_element_type=F32)
    return mixed, largest + jnp.log(total)


def attention_backward(queries, key_rows, value_rows, segments, log_totals, mixed_grad):
    allowed = (segments[:, None] == segments[None, :])[None]
    scale = 1.0 / math.sqrt(HEAD_DIM)
    weights = jnp.exp(masked_scores(queries, key_rows, allowed) - log_totals)
    value_grad = jnp.einsum(
        "hqk,qhe->khe", weights.astype(BF16), mixed_grad, preferred_element_type=F32
    )
    weight_grad = jnp.einsum("qhe,khe->hqk", mixed_grad, value_rows, preferred_element_type=F32)
    inner = jnp.sum(weights * weight_grad, -1, keepdims=True)
    score_grad = (weights * (weight_grad - inner)).astype(BF16)
    query_grad = (
        jnp.einsum("hqk,khe->qhe", score_grad, key_rows, preferred_element_type=F32) * scale
    )
    key_grad = jnp.einsum("hqk,qhe->khe", score_grad, queries, preferred_element_type=F32) * scale
    return query_grad, key_grad, value_grad


def gated_unit(gate, up):
    return jax.nn.gelu(gate, approximate=False) * up


def forward_layer(inputs, segments, tables, params):
    attention_gain, attention_in, attention_out, feedforward_gain, gate_up, down = params
    hidden = gate_up.shape[-1] // 2
    normed = gather_rows(layer_norm(inputs, attention_gain))
    length = normed.shape[0]
    projected = dot(normed, attention_in).reshape(length, 3, -1, HEAD_DIM)
    queries = rotate(projected[:, 0], *tables).astype(BF16)
    key_rows = rotate(projected[:, 1], *tables).astype(BF16)
    value_rows = projected[:, 2].astype(BF16)
    mixed, log_totals = attention_forward(queries, key_rows, value_rows, segments)
    mixed = mixed.astype(BF16).reshape(length, -1)
    middle = inputs + scatter_rows(dot(mixed, attention_out).astype(BF16))
    hidden_in = gather_rows(layer_norm(middle, feedforward_gain))
    gates = dot(hidden_in, gate_up)
    activated = gated_unit(gates[:, :hidden], gates[:, hidden:]).astype(BF16)
    result = middle + scatter_rows(dot(activated, down).astype(BF16))
    kept = (
        inputs, normed, queries, key_rows, value_rows, log_totals, mixed, middle, hidden_in,
        gates, activated,
    )
    return result, kept


def backward_layer(out_grad, segments, tables, params, kept):
    attention_gain, attention_in, attention_out, feedforward_gain, gate_up, down = params
    (
        inputs, normed, queries, key_rows, value_rows, log_totals, mixed, middle, hidden_in,
        gates, activated,
    ) = kept
    hidden = gate_up.shape[-1] // 2
    length, heads, width = queries.shape
    down_in = gather_rows(out_grad.astype(BF16))
    grad_down = dot_tn(activated, down_in)
    activated_grad = dot_nt(down_in, down)
    _, gated_back = jax.vjp(gated_unit, gates[:, :hidden], gates[:, hidden:])
    gates_grad = jnp.concatenate(gated_back(activated_grad), 1).astype(BF16)
    grad_gate_up = dot_tn(hidden_in, gates_grad)
    hidden_grad = scatter_rows(dot_nt(gates_grad, gate_up).astype(BF16))
    middle_part, grad_feedforward_gain = norm_back(middle, feedforward_gain, hidden_grad)
    middle_grad = out_grad + middle_part
    branch_in = gather_rows(middle_grad.astype(BF16))
    grad_attention_out = dot_tn(mixed, branch_in)
    mixed_grad = dot_nt(branch_in, attention_out).astype(BF16).reshape(length, heads, width)
    query_grad, key_grad, value_grad = attention_backward(
        queries, key_rows, value_rows, segments, log_totals, mixed_grad
    )
    cosine, sine_table = tables
    projected_grad = jnp.stack(
        [
            rotate(query_grad, cosine, -sine_table),
            rotate(key_grad, cosine, -sine_table),
            value_grad,
        ],
        1,
    )
    projected_grad = projected_grad.reshape(length, 3 * heads * width).astype(BF16)
    grad_attention_in = dot_tn(normed, projected_grad)
    normed_grad = scatter_rows(dot_nt(projected_grad, attention_in).astype(BF16))
    input_part, grad_attention_gain = norm_back(inputs, attention_gain, normed_grad)
    gains = jnp.stack([grad_attention_gain, grad_feedforward_gain])
    matrices = (grad_attention_in, grad_attention_out, grad_gate_up, grad_down)
    return middle_grad + input_part, gains, matrices


def body(
    layer_input,
    cotangent,
    segment_ids,
    positions,
    attention_gain,
    attention_in_weight,
    attention_out_weight,
    feedforward_gain,
    gate_up_weight,
    down_weight,
):
    core = lax.axis_index("section")
    first = core == 0
    t = lax.axis_index("tensor")

    def mine(pair):
        return jnp.where(first, pair[0], pair[1])

    segments = slot_order(mine(segment_ids[:, 0]), t)
    tables = rotary_tables(slot_order(mine(positions[:, 0]), t))

    def both_layers(own):
        other = swap(own)
        return (jnp.where(first, own, other), jnp.where(first, other, own))

    rows = attention_in_weight.shape[1]
    weights = [
        both_layers(lax.all_gather(w, "dp", axis=0, tiled=True))
        for w in (
            attention_in_weight.reshape(rows, -1),
            attention_out_weight[0],
            gate_up_weight.reshape(rows, -1),
            down_weight[0],
        )
    ]
    gains = [both_layers(attention_gain[0]), both_layers(feedforward_gain[0])]
    params = [
        (gains[0][s], weights[0][s], weights[1][s], gains[1][s], weights[2][s], weights[3][s])
        for s in range(2)
    ]
    state = mine(layer_input[:, 0]).astype(F32)
    kept, results = [], []
    for s in range(2):
        result, saved = forward_layer(state, segments, tables, params[s])
        low = result.astype(BF16)
        results.append(low)
        kept.append(saved)
        state = low.astype(F32)
    grad = mine(cotangent[:, 0]).astype(F32)
    grads, gain_terms, matrix_terms = [None, None], [None, None], [None, None]
    for s in (1, 0):
        grad, gain_terms[s], matrix_terms[s] = backward_layer(
            grad, segments, tables, params[s], kept[s]
        )
        grads[s] = grad.astype(BF16)
        grad = grads[s].astype(F32)

    def own_layer(pair):
        own = jnp.where(first, pair[0], pair[1])
        other = swap(jnp.where(first, pair[1], pair[0]))
        return own, other

    def stacked(pair):
        own, other = own_layer(pair)
        return jnp.stack([jnp.where(first, own, other), jnp.where(first, other, own)])

    hidden_states = stacked(results)[None, :, None]
    input_grads = stacked(grads).astype(F32)[None, :, None]
    own, other = own_layer(gain_terms)
    gain_sums = lax.psum_scatter(own + other, ("tensor", "dp"), scatter_dimension=1, tiled=True)
    shards = []
    for k in range(4):
        own, other = own_layer(
            [matrix_terms[0][k].astype(BF16), matrix_terms[1][k].astype(BF16)]
        )
        total = (own.astype(F32) + other.astype(F32)).astype(BF16)
        shards.append(
            lax.psum_scatter(total, "dp", scatter_dimension=0, tiled=True).astype(F32)
        )
    return (
        hidden_states,
        input_grads,
        gain_sums[:1],
        shards[0].reshape(attention_in_weight.shape),
        shards[1][None],
        gain_sums[1:],
        shards[2].reshape(gate_up_weight.shape),
        shards[3][None],
    )


def solution(mesh):
    return jax.shard_map(
        body,
        mesh=mesh,
        in_specs=(
            P(None, "dp", "tensor", None),
            P(None, "dp", "tensor", None),
            P(None, "dp", None),
            P(None, "dp", None),
            P("section", None),
            P("section", "dp", None, "tensor"),
            P("section", ("tensor", "dp"), None),
            P("section", None),
            P("section", "dp", None, "tensor"),
            P("section", ("tensor", "dp"), None),
        ),
        out_specs=(
            P("section", None, "dp", "tensor", None),
            P("section", None, "dp", "tensor", None),
            P("section", ("tensor", "dp")),
            P("section", "dp", None, "tensor"),
            P("section", ("tensor", "dp"), None),
            P("section", ("tensor", "dp")),
            P("section", "dp", None, "tensor"),
            P("section", ("tensor", "dp"), None),
        ),
        check_vma=False,
    )
```
